128 devices in a mesh: gx: 8 (over z, x_lo), gy: 4 (over x_hi, core), ha: 4 (over y).
Axes of the slice: x: 4 (x_hi: 2, x_lo: 2; x = x_hi * 2 + x_lo), y: 4, z: 4, core: 2. Of those that a mesh axis runs over, the one named last changes fastest.
Arguments:
- tokens: bfloat16 [64, 64, 16, 384], P('gx', 'gy'), may hold values from -30 to 30
- input_weight: bfloat16 [384, 768], P(None, 'ha'), may hold values from -1 to 1
- output_weight: bfloat16 [256, 384], P('ha'), may hold values from -0.375 to 0.375
- tissue_bits: int32 [64, 64], P('gx', 'gy'), may hold values from 0 to 65535
- cotangent: bfloat16 [64, 64, 16, 384], P('gx', 'gy'), may hold values from -6 to 6
Outputs:
- token_gradient: bfloat16 [64, 64, 16, 384], P('gx', 'gy', None, 'ha')
- input_gradient: float32 [384, 768], P(None, 'ha')
- output_gradient: float32 [256, 384], P('ha')
The draws below stay inside these ranges and needn't reach their ends.
All inputs are finite; a program needn't handle non-finite values.
Results may differ from the reference program's by a relative error of at most 0.018.
The reference program's roundings to bfloat16 on the way count: a program that leaves them out, or rounds other values in their place, can miss the bound.
Values may be sent and summed in bfloat16 or wider, within the bound.
No kernel may reach another device: no remote copies, remote signals or barrier semaphores. Data moves between devices by JAX's collectives and lax.ppermute only.
A program may use at most 128 MiB of HBM per device.

```python
import jax
import jax.numpy as jnp
from jax import lax

D = 384
HEADS = 4
HD = 64
REACH = 3
DEPTH = 16
NX = 64
NY = 64
TOKENS = 65536


def draw_tokens(key, part):
    streams = jax.random.split(key, 1)
    base = jax.random.truncated_normal(streams[0], -4.0, 4.0, (NX, NY, DEPTH, D), jnp.float32)
    values = base
    return values.astype(jnp.bfloat16)


def draw_input_weight(key, part):
    base = jax.random.truncated_normal(key, -4.0, 4.0, (D, HEADS, 3, HD), jnp.float32) * D ** (-0.5)
    return base.reshape(D, HEADS * 3 * HD).astype(jnp.bfloat16)


def touch_ends(values, own_key, least, largest):
    place = [jax.random.randint(jax.random.fold_in(own_key, axis), (), 0, length) for axis, length in enumerate(values.shape)]
    longest = values.shape.index(max(values.shape))
    next_to = place[:longest] + [(place[longest] + 1) % values.shape[longest]] + place[longest + 1:]
    return values.at[tuple(place)].set(least).at[tuple(next_to)].set(largest)


def block_levels(own_key, dims, cuts, smallest, top_value):
    def one(axis_at, shards_of):
        draws = jax.random.uniform(jax.random.fold_in(jax.random.fold_in(own_key, 6), axis_at), (shards_of,), jnp.float32, smallest / len(cuts), top_value / len(cuts))
        return jnp.repeat(jnp.exp(draws), dims[axis_at] // shards_of).reshape((-1,) + (1,) * (len(dims) - axis_at - 1))

    loudness = one(*cuts[0])
    for cut in cuts[1:]:
        loudness = loudness * one(*cut)
    return loudness


def normal_values(own_key, extent, width, limit, cuts=(), kind=jnp.bfloat16):
    values = width * jax.random.normal(own_key, extent, jnp.float32)
    if cuts:
        values = values * block_levels(own_key, extent, cuts, -0.22, 0.18)
    return jnp.clip(values, -limit, limit).astype(kind)


def setup_inputs(seed: int = 0) -> dict:
    key_of = jax.random.split(jax.random.key(seed), 6)
    tokens = draw_tokens(jax.random.fold_in(key_of[5], 71), 0)
    input_weight = draw_input_weight(jax.random.fold_in(key_of[5], 71), 0)
    output_weight = normal_values(key_of[2], (HEADS * HD, D), (HEADS * HD) ** -0.5, 0.375, ((0, 4),))
    tissue_bits = touch_ends(jax.random.randint(key_of[3], (NX, NY), 0, 2 ** DEPTH), jax.random.fold_in(key_of[3], 1), 0, (2 ** DEPTH) - 1).astype(jnp.int32)
    cotangent = normal_values(key_of[4], (NX, NY, DEPTH, D), 1.0, 6.0, ((0, 8), (1, 4)))
    return dict(tokens=tokens, input_weight=input_weight, output_weight=output_weight, tissue_bits=tissue_bits, cotangent=cotangent)


def attend_head(entry, valid_padded):
    queries, keys, values, upstream = entry
    score_scale = HD ** -0.5
    window = 2 * REACH + 1
    pads = ((REACH, REACH), (REACH, REACH), (REACH, REACH), (0, 0))
    keys_padded = jnp.pad(keys, pads)
    values_padded = jnp.pad(values, pads)
    offset_index = jnp.arange(window ** 3, dtype=jnp.int32)
    offsets = jnp.stack([offset_index // (window * window), (offset_index // window) % window, offset_index % window], axis=1).astype(jnp.int32)
    centre = REACH * window * window + REACH * window + REACH
    query_float = queries.astype(jnp.float32)
    upstream_float = upstream.astype(jnp.float32)
    anchor = jnp.zeros((), jnp.int32)

    def shifted(array, offset):
        return lax.dynamic_slice(array, (offset[0], offset[1], offset[2], anchor), (NX, NY, DEPTH, HD))

    def score_at(pair):
        offset, position = pair
        keys_here = shifted(keys_padded, offset).astype(jnp.float32)
        scores = jnp.sum(query_float * keys_here, axis=-1) * score_scale
        live = lax.dynamic_slice(valid_padded, (offset[0], offset[1], offset[2]), (NX, NY, DEPTH)) > 0
        return jnp.where(live | (position == centre), scores, -jnp.inf)

    scores = lax.map(score_at, (offsets, offset_index))
    row_max = jnp.max(scores, axis=0)
    raised = jnp.exp(scores - row_max)
    totals = jnp.sum(raised, axis=0)
    weights = (raised / totals).astype(jnp.bfloat16)

    def accumulate(running, pair):
        offset, weight = pair
        values_here = shifted(values_padded, offset).astype(jnp.float32)
        return running + weight.astype(jnp.float32)[..., None] * values_here, None

    output, _ = lax.scan(accumulate, jnp.zeros((NX, NY, DEPTH, HD), jnp.float32), (offsets, weights))
    attended = output.astype(jnp.bfloat16)
    row_inner = jnp.sum(upstream_float * output, axis=-1)
    padded_shape = (NX + 2 * REACH, NY + 2 * REACH, DEPTH + 2 * REACH, HD)

    def backward(carry, pair):
        query_sum, key_sum, value_sum = carry
        offset, weight = pair
        keys_here = shifted(keys_padded, offset).astype(jnp.float32)
        values_here = shifted(values_padded, offset).astype(jnp.float32)
        weight_here = weight.astype(jnp.float32)
        weight_gradient = jnp.sum(upstream_float * values_here, axis=-1)
        score_gradient = lax.optimization_barrier((weight_here * (weight_gradient - row_inner) * score_scale).astype(jnp.bfloat16)).astype(jnp.float32)
        query_sum = query_sum + score_gradient[..., None] * keys_here
        first = (offset[0], offset[1], offset[2], anchor)
        key_sum = lax.dynamic_update_slice(key_sum, shifted(key_sum, offset) + score_gradient[..., None] * query_float, first)
        value_sum = lax.dynamic_update_slice(value_sum, shifted(value_sum, offset) + weight_here[..., None] * upstream_float, first)
        return (query_sum, key_sum, value_sum), None

    start = (jnp.zeros((NX, NY, DEPTH, HD), jnp.float32), jnp.zeros(padded_shape, jnp.float32), jnp.zeros(padded_shape, jnp.float32))
    (query_sum, key_sum, value_sum), _ = lax.scan(backward, start, (offsets, weights))
    key_inner = key_sum[REACH:REACH + NX, REACH:REACH + NY, REACH:REACH + DEPTH]
    value_inner = value_sum[REACH:REACH + NX, REACH:REACH + NY, REACH:REACH + DEPTH]
    return attended, query_sum, key_inner, value_inner


def heads_leading(array):
    return jnp.moveaxis(array, 3, 0)


def reference(tokens, input_weight, output_weight, tissue_bits, cotangent):
    flat_tokens = tokens.reshape(TOKENS, D)
    flat_cotangent = cotangent.reshape(TOKENS, D)
    projected = jnp.dot(flat_tokens, input_weight, preferred_element_type=jnp.float32).astype(jnp.bfloat16)
    projected = projected.reshape(NX, NY, DEPTH, HEADS, 3, HD)
    upstream = jnp.dot(flat_cotangent, output_weight.T, preferred_element_type=jnp.float32).astype(jnp.bfloat16)
    upstream = upstream.reshape(NX, NY, DEPTH, HEADS, HD)
    bit_values = 2 ** jnp.arange(DEPTH, dtype=jnp.int32)
    key_valid = ((tissue_bits[:, :, None] // bit_values) % 2).astype(jnp.float32)
    valid_padded = jnp.pad(key_valid, REACH)

    def one_head(entry):
        return attend_head(entry, valid_padded)

    entries = (heads_leading(projected[:, :, :, :, 0, :]), heads_leading(projected[:, :, :, :, 1, :]), heads_leading(projected[:, :, :, :, 2, :]), heads_leading(upstream))
    attended, query_grads, key_grads, value_grads = lax.map(one_head, entries)
    stacked = jnp.stack([query_grads, key_grads, value_grads], axis=4)
    dprojected = jnp.moveaxis(stacked, 0, 3).astype(jnp.bfloat16).reshape(TOKENS, HEADS * 3 * HD)
    attended_flat = jnp.moveaxis(attended, 0, 3).reshape(TOKENS, HEADS * HD)
    token_gradient = jnp.dot(dprojected, input_weight.T, preferred_element_type=jnp.float32).astype(jnp.bfloat16)
    token_gradient = token_gradient.reshape(NX, NY, DEPTH, D)
    normaliser = TOKENS ** -0.5
    input_gradient = jnp.dot(flat_tokens.T, dprojected, preferred_element_type=jnp.float32) * normaliser
    output_gradient = jnp.dot(attended_flat.T, flat_cotangent, preferred_element_type=jnp.float32) * normaliser
    return token_gradient, input_gradient, output_gradient
```

```python
import jax
import jax.numpy as jnp
from jax import lax
from jax.experimental import pallas as pl
from jax.experimental.pallas import tpu as pltpu
from jax.sharding import PartitionSpec as P

HD = 64
REACH = 3
LANES = 128
BLOCK = 4
SPAN = BLOCK + 2 * REACH
BIG = 2.0**100
F32 = jnp.float32
BF16 = jnp.bfloat16
LANE_X = 64
LANE_Y = 72
LANE_Z = 88
LANE_F = 104

SIDES = ((-1, 0), (1, 0), (0, -1), (0, 1), (-1, -1), (-1, 1), (1, -1), (1, 1))


def dot(a, b):
    return lax.dot_general(a, b, (((1,), (0,)), ((), ())), preferred_element_type=F32)


def dot_t(a, b):
    return lax.dot_general(a, b, (((1,), (1,)), ((), ())), preferred_element_type=F32)


def edge(step, extent):
    if step < 0:
        return 0, REACH
    if step > 0:
        return extent - REACH, extent
    return 0, extent


def halo(step, extent):
    if step < 0:
        return 0, REACH
    if step > 0:
        return extent + REACH, extent + 2 * REACH
    return REACH, extent + REACH


def project_kernel(tok, cot, w, wo, bits, kv_o, qu_o, flags_o, *sends):
    nx, ny, nz, _ = kv_o.shape
    model = tok.shape[-1]
    weight = w[...]
    wide = jnp.concatenate(
        [weight[:, HD:], weight[:, :HD], jnp.zeros((model, HD), BF16)], axis=1
    )
    out_w = jnp.concatenate([jnp.zeros((HD, model), BF16), wo[...]], axis=0)
    z = lax.broadcasted_iota(jnp.int32, (nz, LANES), 0)
    flags = (lax.shift_right_logical(jnp.broadcast_to(bits[...], (nz, LANES)), z) & 1).astype(F32)
    flags = flags.astype(BF16)
    flags_o[...] = flags
    rows = ny * nz
    for x in range(nx):
        part = dot(tok[x * rows : (x + 1) * rows, :], wide)
        ups = dot_t(cot[x * rows : (x + 1) * rows, :], out_w)
        kv_o[x] = part[:, :LANES].astype(BF16).reshape(ny, nz, LANES)
        qu_o[x] = (part[:, LANES:] + ups).astype(BF16).reshape(ny, nz, LANES)
    for (sx, sy), out in zip(SIDES, sends):
        x0, x1 = edge(sx, nx)
        y0, y1 = edge(sy, ny)
        n = y1 - y0
        for x in range(x0, x1):
            out[(x - x0) * n : (x - x0 + 1) * n] = kv_o[x, y0:y1]
        out[(x1 - x0) * n] = flags


def attend_kernel(kv, qu, flags, *refs):
    recvs, refs = refs[:8], refs[8:]
    qa_o, dkv_o = refs[:2]
    backs, refs = refs[2:10], refs[10:]
    kvx, kaug, dkv, s_scr, p_scr, d_scr = refs
    nx, ny, nz, _ = kv.shape
    wx, wy = nx + 2 * REACH, ny + 2 * REACH

    lane = lax.broadcasted_iota(jnp.int32, (nz, LANES), 1)
    zrow = lax.broadcasted_iota(jnp.int32, (nz, LANES), 0)
    low = lane < HD
    far_z = (lane >= LANE_Z) & (lane < LANE_Z + nz) & (jnp.abs(lane - LANE_Z - zrow) > REACH)
    base_z = jnp.where(far_z, -BIG, 0.0).astype(F32)

    def base_of(first, extent, at):
        mine = (lane >= first) & (lane < first + extent)
        return jnp.where(mine & (jnp.abs(lane - first - (at - REACH)) > REACH), -BIG, 0.0)

    base_x = [base_of(LANE_X, nx, x) for x in range(wx)]
    base_y = [base_of(LANE_Y, ny, y) + base_z for y in range(wy)]

    def place(source, group, flag, sy, kx, ky):
        tile = source[group] if isinstance(group, int) else source[group[0], group[1]]
        kvx[kx, ky] = tile
        bias = base_x[kx] + base_y[ky] + jnp.where(lane == LANE_F + sy, flag, 0.0)
        kaug[kx, ky] = jnp.where(low, tile, bias.astype(BF16))

    def rolled(tile, x):
        shift = (LANE_F - x * ny) % LANES
        value = (tile.astype(F32) - 1.0) * BIG
        return pltpu.roll(value, shift, 1) if shift else value

    own = flags[...]
    for x in range(nx):
        plane = rolled(own, x)
        for y in range(ny):
            place(kv, (x, y), plane, y, x + REACH, y + REACH)
    for (sx, sy), piece in zip(SIDES, recvs):
        x0, x1 = edge(sx, nx)
        y0, y1 = edge(sy, ny)
        n = y1 - y0
        hx = halo(-sx, nx)[0]
        hy = halo(-sy, ny)[0]
        tile = piece[(x1 - x0) * n]
        for x in range(x0, x1):
            plane = rolled(tile, x)
            for y in range(y0, y1):
                place(piece, (x - x0) * n + y - y0, plane, y, hx + x - x0, hy + y - y0)

    dkv[...] = jnp.zeros(dkv.shape, F32)
    rows = BLOCK * BLOCK * nz
    keys = SPAN * nz
    qlane = lax.broadcasted_iota(jnp.int32, (rows, LANES), 1)
    qrow = lax.broadcasted_iota(jnp.int32, (rows, LANES), 0)
    strip = BLOCK * nz
    drow = lax.broadcasted_iota(jnp.int32, (strip, rows), 0)
    dlane = lax.broadcasted_iota(jnp.int32, (strip, rows), 1)
    blocks_y = ny // BLOCK
    scale = HD ** (-0.5)

    def one(index, carry):
        x0 = index // blocks_y * BLOCK
        y0 = index % blocks_y * BLOCK
        both = qu[pl.ds(x0, BLOCK), pl.ds(y0, BLOCK)].reshape(rows, LANES)
        qx = x0 + qrow // strip
        qy = y0 + qrow // nz % BLOCK
        hot = (
            (qlane == LANE_X + qx)
            | (qlane == LANE_Y + qy)
            | (qlane == LANE_Z + qrow % nz)
            | ((qlane >= LANE_F) & (qlane < LANE_F + ny))
        )
        wide = both.astype(F32)
        qlow = qlane < HD
        scaled = jnp.where(qlow, wide * scale, 0.0)
        ups = jnp.where(qlow, 0.0, wide)
        aug = jnp.where(qlow, scaled, jnp.where(hot, 1.0, 0.0))
        aug_t = aug.T.astype(BF16)
        q_t = scaled.T.astype(BF16)
        u_t32 = ups.T
        u_t = u_t32.astype(BF16)
        mixed = jnp.concatenate([scaled.astype(BF16), ups.astype(BF16)], axis=0)

        top = jnp.full((8, rows), -jnp.inf, F32)
        for j in range(SPAN):
            s = dot(kaug[x0 + j, pl.ds(y0, SPAN)].reshape(keys, LANES), aug_t)
            if REACH <= j < REACH + BLOCK:
                mid = kvx[x0 + j, pl.ds(y0 + REACH, BLOCK)].reshape(strip, LANES)
                plain = dot(mid, q_t)
                diagonal = dlane - (j - REACH) * strip == drow
                a, b = REACH * nz, REACH * nz + strip
                s = jnp.concatenate([s[:a], jnp.where(diagonal, plain, s[a:b]), s[b:]], axis=0)
            s_scr[j] = s
            top = jnp.maximum(top, jnp.max(s.reshape(keys // 8, 8, rows), axis=0))
        top = jnp.max(top, axis=0, keepdims=True)
        total = jnp.zeros((8, rows), F32)
        for j in range(SPAN):
            e = jnp.exp(s_scr[j] - top)
            s_scr[j] = e
            total = total + jnp.sum(e.reshape(keys // 8, 8, rows), axis=0)
        inverse = 1.0 / jnp.sum(total, axis=0, keepdims=True)
        for j in range(SPAN):
            p_scr[j * keys : (j + 1) * keys] = (s_scr[j] * inverse).astype(BF16)
        block = kvx[pl.ds(x0, SPAN), pl.ds(y0, SPAN)].reshape(SPAN * keys, LANES)
        block_t = block.T
        o_t = dot(block_t[HD:], p_scr[...])
        r = jnp.sum(u_t32[HD:] * o_t, axis=0, keepdims=True)
        for j in range(SPAN):
            kvj = kvx[x0 + j, pl.ds(y0, SPAN)].reshape(keys, LANES)
            g = dot(kvj, u_t)
            p = p_scr[j * keys : (j + 1) * keys]
            ds = (p.astype(F32) * (g - r)).astype(BF16)
            d_scr[j * keys : (j + 1) * keys] = ds
            both_grad = dot(jnp.concatenate([ds, p], axis=1), mixed)
            dkv[x0 + j, pl.ds(y0, SPAN)] += both_grad.reshape(SPAN, nz, LANES)
        q_grad = dot(block_t[:HD], d_scr[...]) * scale
        result = jnp.concatenate([q_grad, o_t], axis=0).T
        qa_o[pl.ds(x0, BLOCK), pl.ds(y0, BLOCK)] = result.astype(BF16).reshape(
            BLOCK, BLOCK, nz, LANES
        )
        return carry

    lax.fori_loop(0, (nx // BLOCK) * blocks_y, one, 0)

    for x in range(nx):
        dkv_o[x] = dkv[x + REACH, REACH : REACH + ny]
    for (sx, sy), out in zip(SIDES, backs):
        x0, x1 = halo(sx, nx)
        y0, y1 = halo(sy, ny)
        n = y1 - y0
        for x in range(x0, x1):
            out[(x - x0) * n : (x - x0 + 1) * n] = dkv[x, y0:y1].astype(BF16)


def tail_kernel(place, qa, dkv, tok, cot, w, *refs):
    recvs, refs = refs[:8], refs[8:]
    own_o, sends, sums_o, acc, grads = refs[0], refs[1:-3], refs[-3], refs[-2], refs[-1]
    nx, ny, nz, _ = dkv.shape
    acc[...] = dkv[...]
    for (sx, sy), piece in zip(SIDES, recvs):
        x0, x1 = edge(-sx, nx)
        y0, y1 = edge(-sy, ny)
        n = y1 - y0
        for x in range(x0, x1):
            acc[x, y0:y1] += piece[(x - x0) * n : (x - x0 + 1) * n].astype(F32)
    rows = nx * ny * nz
    grads[:, :LANES] = acc[...].reshape(rows, LANES).astype(BF16)
    grads[:, LANES:] = qa[...].reshape(rows, LANES)
    parts = w.shape[0]
    mine = place[0]

    def share(step):
        chunk = w[lax.rem(mine + step, parts)]
        wide = jnp.concatenate(
            [chunk[:, HD:], chunk[:, :HD], jnp.zeros((chunk.shape[0], HD), BF16)], axis=1
        )
        return dot_t(grads[...], wide)

    for step in range(1, parts):
        sends[step - 1][...] = share(step).astype(BF16)
    own_o[...] = share(0)
    grads_t = grads[...].T
    sums_o[: 3 * HD] = dot(grads_t[: 3 * HD], tok[...]).astype(BF16)
    sums_o[3 * HD :] = dot(grads_t[3 * HD :], cot[...]).astype(BF16)


def moved(pieces, reverse):
    nx, ny = lax.axis_size("gx"), lax.axis_size("gy")
    out = []
    for (sx, sy), piece in zip(SIDES, pieces):
        pairs = []
        for x in range(nx):
            for y in range(ny):
                if 0 <= x + sx < nx and 0 <= y + sy < ny:
                    pairs.append((x * ny + y, (x + sx) * ny + y + sy))
        out.append(lax.ppermute(piece, ("gx", "gy"), pairs))
    return out


def call(kernel, outs, scratch=(), scalars=0, count=0):
    vmem = pl.BlockSpec(memory_space=pltpu.VMEM)
    smem = pl.BlockSpec(memory_space=pltpu.SMEM)
    return pl.pallas_call(
        kernel,
        out_shape=outs,
        in_specs=[smem] * scalars + [vmem] * (count - scalars),
        out_specs=[vmem] * len(outs),
        scratch_shapes=list(scratch),
        compiler_params=pltpu.CompilerParams(vmem_limit_bytes=56 << 20),
    )


def shards(tokens, input_weight, output_weight, tissue_bits, cotangent):
    nx, ny, nz, model = tokens.shape
    rows = nx * ny * nz
    wx, wy = nx + 2 * REACH, ny + 2 * REACH
    flat_tokens = tokens.reshape(rows, model)
    flat_cotangent = cotangent.reshape(rows, model)
    shape = jax.ShapeDtypeStruct
    sizes = []
    for sx, sy in SIDES:
        x0, x1 = edge(sx, nx)
        y0, y1 = edge(sy, ny)
        sizes.append((x1 - x0) * (y1 - y0))
    kv, qu, flags, *sends = call(
        project_kernel,
        [shape((nx, ny, nz, LANES), BF16)] * 2
        + [shape((nz, LANES), BF16)]
        + [shape((n + 1, nz, LANES), BF16) for n in sizes],
        count=5,
    )(flat_tokens, flat_cotangent, input_weight, output_weight, tissue_bits.reshape(1, nx * ny))
    recvs = moved(sends, False)
    span_rows = SPAN * SPAN * nz
    block_rows = BLOCK * BLOCK * nz
    qa, dkv, *backs = call(
        attend_kernel,
        [shape((nx, ny, nz, LANES), BF16), shape((nx, ny, nz, LANES), F32)]
        + [shape((n, nz, LANES), BF16) for n in sizes],
        scratch=[
            pltpu.VMEM((wx, wy, nz, LANES), BF16),
            pltpu.VMEM((wx, wy, nz, LANES), BF16),
            pltpu.VMEM((wx, wy, nz, LANES), F32),
            pltpu.VMEM((SPAN, SPAN * nz, block_rows), F32),
            pltpu.VMEM((span_rows, block_rows), BF16),
            pltpu.VMEM((span_rows, block_rows), BF16),
        ],
        count=11,
    )(kv, qu, flags, *recvs)
    returned = moved(backs, True)
    parts = lax.axis_size("ha")
    width = model // parts
    mine = lax.axis_index("ha").astype(jnp.int32).reshape(1)
    own, *rest = call(
        tail_kernel,
        [shape((rows, width), F32)]
        + [shape((rows, width), BF16)] * (parts - 1)
        + [shape((4 * HD, model), BF16)],
        scratch=[pltpu.VMEM((nx, ny, nz, LANES), F32), pltpu.VMEM((rows, 2 * LANES), BF16)],
        scalars=1,
        count=14,
    )(
        mine,
        qa,
        dkv,
        flat_tokens,
        flat_cotangent,
        input_weight.reshape(parts, width, 3 * HD),
        *returned,
    )
    shares, sums = rest[:-1], rest[-1]
    total = own
    for step, piece in zip(range(1, parts), shares):
        ring = [(i, (i + step) % parts) for i in range(parts)]
        total = total + lax.ppermute(piece, "ha", ring).astype(F32)
    token_gradient = total.astype(BF16).reshape(nx, ny, nz, width)
    grid = ("gx", "gy")
    members = lax.axis_size("gx") * lax.axis_size("gy")
    split = sums.reshape(members, 4 * HD // members, model)
    met = lax.all_to_all(split, grid, 0, 0, tiled=True)
    mean = jnp.sum(met.astype(F32), axis=0, keepdims=True).astype(BF16)
    spread = lax.all_to_all(jnp.broadcast_to(mean, split.shape), grid, 0, 0, tiled=True)
    normaliser = (rows * members) ** (-0.5)
    whole = spread.reshape(4 * HD, model).astype(F32) * normaliser
    input_gradient = jnp.concatenate([whole[2 * HD : 3 * HD], whole[: 2 * HD]], axis=0).T
    return token_gradient, input_gradient, whole[3 * HD :]


def solution(mesh):
    placed = (
        P("gx", "gy", None, None),
        P(None, "ha"),
        P("ha", None),
        P("gx", "gy"),
        P("gx", "gy", None, None),
    )
    return jax.shard_map(
        shards,
        mesh=mesh,
        in_specs=placed,
        out_specs=(P("gx", "gy", None, "ha"), P(None, "ha"), P("ha", None)),
        check_vma=False,
    )
```

```python
import jax
import jax.numpy as jnp
from jax import lax
from jax.experimental import pallas as pl
from jax.experimental.pallas import tpu as pltpu
from jax.sharding import PartitionSpec as P


HD = 64
REACH = 3
LANES = 128
BLOCK = 4
SPAN = BLOCK + 2 * REACH
BIG = 2.0**100
F32 = jnp.float32
BF16 = jnp.bfloat16
LANE_X = 64
LANE_Y = 72
LANE_Z = 88
LANE_F = 104

STEPS = (-1, 1)


def dot(a, b):
    return lax.dot_general(a, b, (((1,), (0,)), ((), ())), preferred_element_type=F32)


def dot_t(a, b):
    return lax.dot_general(a, b, (((1,), (1,)), ((), ())), preferred_element_type=F32)


def edge(step, extent):
    if step < 0:
        return 0, REACH
    if step > 0:
        return extent - REACH, extent
    return 0, extent


def halo(step, extent):
    if step < 0:
        return 0, REACH
    if step > 0:
        return extent + REACH, extent + 2 * REACH
    return REACH, extent + REACH


def project_kernel(tok, cot, w, wo, bits, kv_o, qu_o, *sends):
    nx, ny, nz, _ = kv_o.shape
    weight = w[...]
    wide = jnp.concatenate(
        [weight[HD:], weight[:HD], jnp.zeros((HD, weight.shape[1]), BF16)], axis=0
    )
    out_w = jnp.concatenate([jnp.zeros((HD, weight.shape[1]), BF16), wo[...]], axis=0)
    z = lax.broadcasted_iota(jnp.int32, (nz, LANES), 0)
    flags = (lax.shift_right_logical(jnp.broadcast_to(bits[...], (nz, LANES)), z) & 1).astype(F32)
    flags = flags.astype(BF16)
    rows = ny * nz
    for x in range(nx):
        part = dot_t(tok[x * rows : (x + 1) * rows, :], wide)
        ups = dot_t(cot[x * rows : (x + 1) * rows, :], out_w)
        kv_o[x] = part[:, :LANES].astype(BF16).reshape(ny, nz, LANES)
        qu_o[x] = (part[:, LANES:] + ups).astype(BF16).reshape(ny, nz, LANES)
    for step, out in zip(STEPS, sends[:2]):
        y0, y1 = edge(step, ny)
        for x in range(nx):
            out[x * REACH : (x + 1) * REACH] = kv_o[x, y0:y1]
        out[nx * REACH] = flags
    sends[2][...] = flags


def pack_kernel(kv, flags, low, high, kvc_o, tags_o, *sends):
    nx, ny, _, _ = kv.shape
    wy = ny + 2 * REACH
    for x in range(nx):
        kvc_o[x, REACH : REACH + ny] = kv[x]
        kvc_o[x, :REACH] = low[x * REACH : (x + 1) * REACH]
        kvc_o[x, REACH + ny :] = high[x * REACH : (x + 1) * REACH]
    tiles = (low[nx * REACH], flags[...], high[nx * REACH])
    for t, tile in enumerate(tiles):
        tags_o[t] = tile
    for step, out in zip(STEPS, sends):
        x0, x1 = edge(step, nx)
        for x in range(x0, x1):
            out[(x - x0) * wy : (x - x0 + 1) * wy] = kvc_o[x]
        for t, tile in enumerate(tiles):
            out[REACH * wy + t] = tile


class Bias:
    def __init__(self, nx, ny, nz):
        self.nx, self.ny, self.nz = nx, ny, nz
        self.lane = lax.broadcasted_iota(jnp.int32, (nz, LANES), 1)
        zrow = lax.broadcasted_iota(jnp.int32, (nz, LANES), 0)
        far = self.mine(LANE_Z, nz) & (jnp.abs(self.lane - LANE_Z - zrow) > REACH)
        base_z = jnp.where(far, -BIG, 0.0).astype(F32)
        self.base_y = [self.base(LANE_Y, ny, y) + base_z for y in range(ny + 2 * REACH)]

    def mine(self, first, extent):
        return (self.lane >= first) & (self.lane < first + extent)

    def base(self, first, extent, at):
        far = jnp.abs(self.lane - first - (at - REACH)) > REACH
        return jnp.where(self.mine(first, extent) & far, -BIG, 0.0)

    def rolled(self, tile, x):
        shift = (LANE_F - x * self.ny) % LANES
        value = (tile.astype(F32) - 1.0) * BIG
        return pltpu.roll(value, shift, 1) if shift else value

    def fill(self, source, tiles, kx, x, target):
        base_x = self.base(LANE_X, self.nx, kx)
        planes = [self.rolled(tile, x) for tile in tiles]
        for y in range(self.ny + 2 * REACH):
            which = 0 if y < REACH else 1 if y < REACH + self.ny else 2
            at = (y - REACH) % self.ny
            flag = jnp.where(self.lane == LANE_F + at, planes[which], 0.0)
            bias = (base_x + self.base_y[y] + flag).astype(BF16)
            target(y, jnp.where(self.lane < HD, source(y), bias))


def block_of(index, ny):
    blocks_y = ny // BLOCK
    half = index // blocks_y
    return half, half * BLOCK, index % blocks_y * BLOCK


def near_planes(half, x0):
    own = [x0 + i for i in range(BLOCK)]
    return own + [BLOCK - REACH * half + i for i in range(REACH)]


def local_kernel(kvc, qu, tags, e_o, stat_o, aug_o, up_o, kaug):
    nx, wy, nz, _ = kvc.shape
    ny = wy - 2 * REACH
    bias = Bias(nx, ny, nz)
    tiles = [tags[t] for t in range(3)]
    for x in range(nx):

        def target(y, value, x=x):
            kaug[x, y] = value

        bias.fill(lambda y, x=x: kvc[x, y], tiles, x + REACH, x, target)
    rows = BLOCK * BLOCK * nz
    keys = SPAN * nz
    strip = BLOCK * nz
    qlane = lax.broadcasted_iota(jnp.int32, (rows, LANES), 1)
    qrow = lax.broadcasted_iota(jnp.int32, (rows, LANES), 0)
    drow = lax.broadcasted_iota(jnp.int32, (strip, rows), 0)
    dlane = lax.broadcasted_iota(jnp.int32, (strip, rows), 1)
    scale = HD ** (-0.5)

    def one(index, carry):
        half, x0, y0 = block_of(index, ny)
        both = qu[pl.ds(x0, BLOCK), pl.ds(y0, BLOCK)].reshape(rows, LANES)
        qx = x0 + qrow // strip
        qy = y0 + qrow // nz % BLOCK
        hot = (
            (qlane == LANE_X + qx)
            | (qlane == LANE_Y + qy)
            | (qlane == LANE_Z + qrow % nz)
            | ((qlane >= LANE_F) & (qlane < LANE_F + ny))
        )
        wide = both.astype(F32)
        qlow = qlane < HD
        scaled = jnp.where(qlow, wide * scale, 0.0)
        aug = jnp.where(qlow, scaled, jnp.where(hot, 1.0, 0.0))
        aug_t = aug.T.astype(BF16)
        q_t = scaled.T.astype(BF16)
        aug_o[index] = aug_t
        up_o[index] = jnp.where(qlow, 0.0, wide).T.astype(BF16)
        top = jnp.full((8, rows), -jnp.inf, F32)
        planes = near_planes(half, x0)
        for j, x in enumerate(planes):
            s = dot(kaug[x, pl.ds(y0, SPAN)].reshape(keys, LANES), aug_t)
            if j < BLOCK:
                mid = kvc[x, pl.ds(y0 + REACH, BLOCK)].reshape(strip, LANES)
                plain = dot(mid, q_t)
                diagonal = dlane - j * strip == drow
                a, b = REACH * nz, REACH * nz + strip
                s = jnp.concatenate([s[:a], jnp.where(diagonal, plain, s[a:b]), s[b:]], axis=0)
            e_o[index, j] = s
            top = jnp.maximum(top, jnp.max(s.reshape(keys // 8, 8, rows), axis=0))
        top = jnp.max(top, axis=0, keepdims=True)
        total = jnp.zeros((8, rows), F32)
        for j in range(len(planes)):
            e = jnp.exp(e_o[index, j] - top)
            e_o[index, j] = e
            total = total + jnp.sum(e.reshape(keys // 8, 8, rows), axis=0)
        stat_o[index, 0] = jnp.broadcast_to(top, (8, rows))
        stat_o[index, 1] = total
        return carry

    lax.fori_loop(0, (nx // BLOCK) * (ny // BLOCK), one, 0)


def mixed_of(qu, x0, y0):
    nz = qu.shape[2]
    rows = BLOCK * BLOCK * nz
    wide = qu[pl.ds(x0, BLOCK), pl.ds(y0, BLOCK)].reshape(rows, LANES).astype(F32)
    qlow = lax.broadcasted_iota(jnp.int32, (rows, LANES), 1) < HD
    scaled = jnp.where(qlow, wide * HD ** (-0.5), 0.0)
    return jnp.concatenate([scaled, jnp.where(qlow, 0.0, wide)], axis=0).astype(BF16)


def far_kernel(kvc, qu, e_i, stat, aug, up, low, high, *refs):
    p_o, r_o, dqo_o = refs[:3]
    backs = refs[3:5]
    kvh, kaug, acc, s_scr, d_scr = refs[5:]
    nx, wy, nz, _ = kvc.shape
    ny = wy - 2 * REACH
    bias = Bias(nx, ny, nz)
    for side, piece in enumerate((low, high)):
        tiles = [piece[REACH * wy + t] for t in range(3)]
        first = halo(STEPS[side], nx)[0]
        own = edge(-STEPS[side], nx)[0]
        for i in range(REACH):
            kvh[side, i] = piece[i * wy : (i + 1) * wy]

            def target(y, value, side=side, i=i):
                kaug[side, i, y] = value

            bias.fill(
                lambda y, i=i, piece=piece: piece[i * wy + y], tiles, first + i, own + i, target
            )
    acc[...] = jnp.zeros(acc.shape, F32)
    rows = BLOCK * BLOCK * nz
    keys = SPAN * nz
    scale = HD ** (-0.5)
    near = BLOCK + REACH

    def one(index, carry):
        half, x0, y0 = block_of(index, ny)
        aug_t = aug[index]
        u_t = up[index]
        mixed = mixed_of(qu, x0, y0)
        before = stat[index, 0, :1]
        top = jnp.full((8, rows), -jnp.inf, F32)
        for i in range(REACH):
            s = dot(kaug[half, i, pl.ds(y0, SPAN)].reshape(keys, LANES), aug_t)
            s_scr[i] = s
            top = jnp.maximum(top, jnp.max(s.reshape(keys // 8, 8, rows), axis=0))
        top = jnp.maximum(jnp.max(top, axis=0, keepdims=True), before)
        shrink = jnp.exp(before - top)
        total = stat[index, 1] * shrink
        for i in range(REACH):
            e = jnp.exp(s_scr[i] - top)
            s_scr[i] = e
            total = total + jnp.sum(e.reshape(keys // 8, 8, rows), axis=0)
        inverse = 1.0 / jnp.sum(total, axis=0, keepdims=True)
        shrunk = shrink * inverse
        for j in range(near):
            p_o[index, j * keys : (j + 1) * keys] = (e_i[index, j] * shrunk).astype(BF16)
        for i in range(REACH):
            j = near + i
            p_o[index, j * keys : (j + 1) * keys] = (s_scr[i] * inverse).astype(BF16)
        planes = near_planes(half, x0)
        block = [kvc[x, pl.ds(y0, SPAN)].reshape(keys, LANES) for x in planes]
        outer = [kvh[half, i, pl.ds(y0, SPAN)].reshape(keys, LANES) for i in range(REACH)]
        block_t = jnp.concatenate(block + outer, axis=0).T
        o_t = dot(block_t[HD:], p_o[index])
        r = jnp.sum(u_t[HD:].astype(F32) * o_t, axis=0, keepdims=True)
        r_o[index] = jnp.broadcast_to(r, (8, rows))
        for i in range(REACH):
            j = near + i
            g = dot(outer[i], u_t)
            p = p_o[index, j * keys : (j + 1) * keys]
            ds = (p.astype(F32) * (g - r)).astype(BF16)
            d_scr[i * keys : (i + 1) * keys] = ds
            grad = dot(jnp.concatenate([ds, p], axis=1), mixed)
            acc[half, i, pl.ds(y0, SPAN)] += grad.reshape(SPAN, nz, LANES)
        dqo_o[index, :HD] = dot(block_t[:HD, near * keys :], d_scr[...]) * scale
        dqo_o[index, HD:] = o_t
        return carry

    lax.fori_loop(0, (nx // BLOCK) * (ny // BLOCK), one, 0)
    for side, out in enumerate(backs):
        for i in range(REACH):
            out[i * wy : (i + 1) * wy] = acc[side, i].astype(BF16)


def near_kernel(kvc, qu, p_i, r_i, up, dqo, qa_o, dkv_o, d_scr):
    nx, wy, nz, _ = kvc.shape
    ny = wy - 2 * REACH
    keys = SPAN * nz
    scale = HD ** (-0.5)
    dkv_o[...] = jnp.zeros(dkv_o.shape, F32)

    def one(index, carry):
        half, x0, y0 = block_of(index, ny)
        u_t = up[index]
        mixed = mixed_of(qu, x0, y0)
        r = r_i[index, :1]
        planes = near_planes(half, x0)
        block = [kvc[x, pl.ds(y0, SPAN)].reshape(keys, LANES) for x in planes]
        for j, x in enumerate(planes):
            g = dot(block[j], u_t)
            p = p_i[index, j * keys : (j + 1) * keys]
            ds = (p.astype(F32) * (g - r)).astype(BF16)
            d_scr[j * keys : (j + 1) * keys] = ds
            grad = dot(jnp.concatenate([ds, p], axis=1), mixed)
            dkv_o[x, pl.ds(y0, SPAN)] += grad.reshape(SPAN, nz, LANES)
        block_t = jnp.concatenate(block, axis=0).T
        q_grad = dot(block_t[:HD], d_scr[...]) * scale + dqo[index, :HD]
        result = jnp.concatenate([q_grad, dqo[index, HD:]], axis=0).T
        qa_o[pl.ds(x0, BLOCK), pl.ds(y0, BLOCK)] = result.astype(BF16).reshape(
            BLOCK, BLOCK, nz, LANES
        )
        return carry

    lax.fori_loop(0, (nx // BLOCK) * (ny // BLOCK), one, 0)


def returned(dkv, pieces, x, y0, y1):
    nx, wy = dkv.shape[:2]
    value = dkv[x, y0:y1]
    for step, piece in zip(STEPS, pieces):
        a, b = edge(step, nx)
        if a <= x < b:
            value = value + piece[(x - a) * wy + y0 : (x - a) * wy + y1].astype(F32)
    return value


def rim_kernel(dkv, low, high, *sends):
    nx, wy = dkv.shape[:2]
    ny = wy - 2 * REACH
    for step, out in zip(STEPS, sends):
        y0, y1 = halo(step, ny)
        for x in range(nx):
            rim = returned(dkv, (low, high), x, y0, y1)
            out[x * REACH : (x + 1) * REACH] = rim.astype(BF16)


def tail_kernel(place, qa, dkv, low, high, tok, cot, w, south, north, *refs):
    own_o, sends, sums_o, grads = refs[0], refs[1:-2], refs[-2], refs[-1]
    nx, ny, nz, _ = qa.shape
    rows = nx * ny * nz
    plane = ny * nz
    for x in range(nx):
        value = returned(dkv, (low, high), x, REACH, REACH + ny)
        parts = []
        for step, piece in zip(STEPS, (south, north)):
            a, b = edge(step, ny)
            parts.append(value[a:b] + piece[x * REACH : (x + 1) * REACH].astype(F32))
        value = jnp.concatenate([parts[0], value[REACH : ny - REACH], parts[1]], axis=0)
        grads[x * plane : (x + 1) * plane, :LANES] = value.reshape(plane, LANES).astype(BF16)
    grads[:, LANES:] = qa[...].reshape(rows, LANES)
    count = w.shape[0]
    mine = place[0]

    def share(step):
        chunk = w[lax.rem(mine + step, count)]
        wide = jnp.concatenate(
            [chunk[:, HD:], chunk[:, :HD], jnp.zeros((chunk.shape[0], HD), BF16)], axis=1
        )
        return dot_t(grads[...], wide)

    for step in range(1, count):
        sends[step - 1][...] = share(step).astype(BF16)
    own_o[...] = share(0)
    grads_t = grads[...].T
    sums_o[: 3 * HD] = dot(grads_t[: 3 * HD], tok[...]).astype(BF16)
    sums_o[3 * HD :] = dot(grads_t[3 * HD :], cot[...]).astype(BF16)


def shifted(pieces, axis):
    count = lax.axis_size(axis)
    up = [(i, i + 1) for i in range(count - 1)]
    down = [(target, source) for source, target in up]
    to_low, to_high = pieces
    from_low = lax.ppermute(to_high, axis, up)
    from_high = lax.ppermute(to_low, axis, down)
    return from_low, from_high


def call(kernel, outs, scratch=(), scalars=0, count=0, limit=20):
    vmem = pl.BlockSpec(memory_space=pltpu.VMEM)
    smem = pl.BlockSpec(memory_space=pltpu.SMEM)
    return pl.pallas_call(
        kernel,
        out_shape=outs,
        in_specs=[smem] * scalars + [vmem] * (count - scalars),
        out_specs=[vmem] * len(outs),
        scratch_shapes=list(scratch),
        compiler_params=pltpu.CompilerParams(vmem_limit_bytes=limit << 20),
    )


def shards(tokens, input_weight, output_weight, tissue_bits, cotangent):
    nx, ny, nz, model = tokens.shape
    rows = nx * ny * nz
    wy = ny + 2 * REACH
    flat_tokens = tokens.reshape(rows, model)
    flat_cotangent = cotangent.reshape(rows, model)
    blocks = (nx // BLOCK) * (ny // BLOCK)
    keys = SPAN * nz
    queries = BLOCK * BLOCK * nz
    near = BLOCK + REACH

    def half(*dims):
        return jax.ShapeDtypeStruct(dims, BF16)

    def full(*dims):
        return jax.ShapeDtypeStruct(dims, F32)

    grid = half(nx, ny, nz, LANES)
    rim_y = REACH * nx
    rim_x = REACH * wy
    kv, qu, y_low, y_high, flags = call(
        project_kernel,
        [grid, grid] + [half(rim_y + 1, nz, LANES)] * 2 + [half(nz, LANES)],
        count=5,
    )(
        flat_tokens,
        flat_cotangent,
        input_weight.T,
        output_weight,
        tissue_bits.reshape(1, nx * ny),
    )
    south, north = shifted((y_low, y_high), "gy")
    kvc, tags, x_low, x_high = call(
        pack_kernel,
        [half(nx, wy, nz, LANES), half(3, nz, LANES)] + [half(rim_x + 3, nz, LANES)] * 2,
        count=4,
    )(kv, flags, south, north)
    west, east = shifted((x_low, x_high), "gx")
    e, stat, aug, up = call(
        local_kernel,
        [
            full(blocks, near, keys, queries),
            full(blocks, 2, 8, queries),
            half(blocks, LANES, queries),
            half(blocks, LANES, queries),
        ],
        scratch=[pltpu.VMEM((nx, wy, nz, LANES), BF16)],
        count=3,
    )(kvc, qu, tags)
    p, r, dqo, back_low, back_high = call(
        far_kernel,
        [
            half(blocks, SPAN * keys, queries),
            full(blocks, 8, queries),
            full(blocks, LANES, queries),
        ]
        + [half(rim_x, nz, LANES)] * 2,
        scratch=[
            pltpu.VMEM((2, REACH, wy, nz, LANES), BF16),
            pltpu.VMEM((2, REACH, wy, nz, LANES), BF16),
            pltpu.VMEM((2, REACH, wy, nz, LANES), F32),
            pltpu.VMEM((REACH, keys, queries), F32),
            pltpu.VMEM((REACH * keys, queries), BF16),
        ],
        count=8,
    )(kvc, qu, e, stat, aug, up, west, east)
    low, high = shifted((back_low, back_high), "gx")
    qa, dkv = call(
        near_kernel,
        [grid, full(nx, wy, nz, LANES)],
        scratch=[pltpu.VMEM((near * keys, queries), BF16)],
        count=6,
    )(kvc, qu, p, r, up, dqo)
    rims = call(rim_kernel, [half(rim_y, nz, LANES)] * 2, count=3)(dkv, low, high)
    south, north = shifted(rims, "gy")
    parts = lax.axis_size("ha")
    width = model // parts
    mine = lax.axis_index("ha").astype(jnp.int32).reshape(1)
    own, *rest = call(
        tail_kernel,
        [full(rows, width)]
        + [half(rows, width)] * (parts - 1)
        + [half(4 * HD, model)],
        scratch=[pltpu.VMEM((rows, 2 * LANES), BF16)],
        scalars=1,
        count=10,
    )(
        mine,
        qa,
        dkv,
        low,
        high,
        flat_tokens,
        flat_cotangent,
        input_weight.reshape(parts, width, 3 * HD),
        south,
        north,
    )
    shares, sums = rest[:-1], rest[-1]
    total = own
    for step, piece in zip(range(1, parts), shares):
        ring = [(i, (i + step) % parts) for i in range(parts)]
        total = total + lax.ppermute(piece, "ha", ring).astype(F32)
    token_gradient = total.astype(BF16).reshape(nx, ny, nz, width)
    both = ("gx", "gy")
    members = lax.axis_size("gx") * lax.axis_size("gy")
    split = sums.reshape(members, 4 * HD // members, model)
    met = lax.all_to_all(split, both, 0, 0, tiled=True)
    mean = jnp.sum(met.astype(F32), axis=0, keepdims=True).astype(BF16)
    spread = lax.all_to_all(jnp.broadcast_to(mean, split.shape), both, 0, 0, tiled=True)
    normaliser = (rows * members) ** (-0.5)
    whole = spread.reshape(4 * HD, model).astype(F32) * normaliser
    input_gradient = jnp.concatenate([whole[2 * HD : 3 * HD], whole[: 2 * HD]], axis=0).T
    return token_gradient, input_gradient, whole[3 * HD :]


def solution(mesh):
    placed = (
        P("gx", "gy", None, None),
        P(None, "ha"),
        P("ha", None),
        P("gx", "gy"),
        P("gx", "gy", None, None),
    )

    return jax.shard_map(
        shards,
        mesh=mesh,
        in_specs=placed,
        out_specs=(P("gx", "gy", None, "ha"), P(None, "ha"), P("ha", None)),
        check_vma=False,
    )
```
